256 devices in a mesh: fsdp: 64 (over z, x, core), tp: 4 (over y).
Axes of the slice: x: 4, y: 4, z: 8, core: 2. Of those that a mesh axis runs over, the one named last changes fastest.
Arguments:
- activations: bfloat16 [8192, 5120], P('fsdp', 'tp'), may hold values from -6 to 6
- out_grad: bfloat16 [8192, 5120], P('fsdp'), may hold values from -0.1875 to 0.1875
- momentum: float32 [5120, 5120], P('fsdp', 'tp'), may hold values from -6 to 6
- right_prev: float32 [5120, 256], P('tp'), may hold values from -6 to 6
Outputs:
- new_momentum: float32 [5120, 5120], P('fsdp', 'tp')
- update: float32 [5120, 5120], P('fsdp', 'tp')
- right_next: float32 [5120, 256], P('tp', 'fsdp')
The draws below stay inside these ranges and needn't reach their ends.
All inputs are finite; a program needn't handle non-finite values.
Results may differ from the reference program's by a relative error of at most 0.0003.
Values sent between devices are 32-bit elements; how exact they have to be, the bound alone decides.
No kernel may reach another device: no remote copies, remote signals or barrier semaphores. Data moves between devices by JAX's collectives and lax.ppermute only.
A program may use at most 128 MiB of HBM per device.

```python
import math
import jax
import jax.numpy as jnp
from jax import lax

D = 5120
R = 256
TOKENS = 8192


def spiked(drawn, stream_key, source, target, parts, factor):
    def block_of(axis_at):
        return (jnp.arange(drawn.shape[axis_at]) // (drawn.shape[axis_at] // parts)).reshape((-1,) + (1,) * (drawn.ndim - 1 - axis_at))

    first = jax.random.permutation(stream_key, parts)[block_of(target)]
    other_side = (block_of(target) + parts // 2) % parts
    return jnp.where((block_of(source) == first) | (block_of(source) == other_side), factor * drawn, drawn)


def level_of(own_key, extent, cuts, smallest, top_value):
    def one(axis_at, shards_of):
        draws = jax.random.uniform(jax.random.fold_in(jax.random.fold_in(own_key, 6), axis_at), (shards_of,), jnp.float32, smallest / len(cuts), top_value / len(cuts))
        return jnp.repeat(jnp.exp(draws), extent[axis_at] // shards_of).reshape((-1,) + (1,) * (len(extent) - axis_at - 1))

    loudness = one(*cuts[0])
    for cut in cuts[1:]:
        loudness = loudness * one(*cut)
    return loudness


def normal_values(rng, extent, deviation, limit, split=(), dtype=jnp.bfloat16):
    level = level_of(rng, extent, split, -0.22, 0.18) if split else 1.0
    array = jax.random.normal(rng, extent, jnp.float32) * deviation * level
    return jnp.minimum(jnp.maximum(array, -limit), limit).astype(dtype)


def noise_with(rng, shape, deviation, reach, split, heavy, kind=jnp.bfloat16):
    values = deviation * jax.random.normal(rng, shape, jnp.float32)
    if split:
        values = values * level_of(rng, shape, split, -0.22, 0.18)
    return jnp.clip(spiked(values, jax.random.fold_in(rng, 3), *heavy), -reach, reach).astype(kind)


def setup_inputs(seed: int = 0) -> dict:
    key_list = jax.random.split(jax.random.key(seed), 5)
    return {
        "activations": normal_values(key_list[0], (TOKENS, D), 1.0, 6.0, ((0, 64), (1, 4))),
        "out_grad": noise_with(key_list[1], (TOKENS, D), (TOKENS ** -0.5), 0.1875, ((0, 64),), (0, 1, 64, 4.0)),
        "momentum": normal_values(key_list[2], (D, D), 1.0, 6.0, ((0, 64), (1, 4)), jnp.float32),
        "right_prev": normal_values(key_list[3], (D, R), 1.0, 6.0, ((0, 4),), jnp.float32),
    }


momentum_decay = 0.95

def reference(activations, out_grad, momentum, right_prev):
    high = lax.Precision.HIGHEST
    grad = lax.dot_general(out_grad.astype(jnp.float32), activations.astype(jnp.float32), (((0,), (0,)), ((), ())), preferred_element_type=jnp.float32)
    buffer = momentum + grad
    left = jnp.dot(buffer, right_prev, precision=high)
    gram = jnp.dot(left.T, left, precision=high)
    lower = jnp.linalg.cholesky(gram)
    basis = lax.linalg.triangular_solve(lower, left, left_side=False, lower=True, transpose_a=True)
    right = jnp.dot(buffer.T, basis, precision=high)
    factor = lax.rsqrt(lax.optimization_barrier(jnp.mean(right * right, axis=0)) + 1e-06)
    right_next = right * factor[None, :]
    new_momentum = buffer - (1.0 - momentum_decay) * jnp.dot(basis, right.T, precision=high)
    update = math.sqrt(D / R) * jnp.dot(basis, right_next.T, precision=high)
    return (new_momentum, update, right_next)
```

```python
import math

import jax
import jax.numpy as jnp
from jax import lax
from jax.experimental import pallas as pl
from jax.experimental.pallas import tpu as pltpu
from jax.sharding import Mesh
from jax.sharding import PartitionSpec as P

D = 5120
R = 256
NZ, NX, NC, NY = 8, 4, 2, 4
FSDP = ("z", "x", "c")
EDGE = 64
HIGH = lax.Precision.HIGHEST

momentum_decay = 0.95


def shifted(v, axis, n, k):
    return lax.ppermute(v, axis, [(i, (i + k) % n) for i in range(n)])


def other_core(v):
    return lax.ppermute(v, "c", [(0, 1), (1, 0)])


def dot(a, b, dims):
    return lax.dot_general(a, b, (dims, ((), ())), precision=HIGH, preferred_element_type=jnp.float32)


def inverse_factor_kernel(gram_ref, out_ref, work_ref):
    def mm(a, b, dims):
        return lax.dot_general(
            a, b, (dims, ((), ())), precision=HIGH, preferred_element_type=jnp.float32
        )

    blocks = R // EDGE
    rows = lax.broadcasted_iota(jnp.int32, (EDGE, 2 * EDGE), 0)
    lanes = lax.broadcasted_iota(jnp.int32, (EDGE, 2 * EDGE), 1)
    eye = (rows + EDGE == lanes).astype(jnp.float32)
    rest_lanes = lax.broadcasted_iota(jnp.int32, (EDGE, R), 1)
    all_rows = lax.broadcasted_iota(jnp.int32, (R, R), 0)
    all_lanes = lax.broadcasted_iota(jnp.int32, (R, R), 1)
    work_ref[:, :R] = gram_ref[...]
    work_ref[:, R:] = (all_rows == all_lanes).astype(jnp.float32)

    def step(i, _):
        here = pl.ds(pl.multiple_of(i * EDGE, EDGE), EDGE)
        state = jnp.where(lanes < EDGE, work_ref[here, : 2 * EDGE], eye)
        pivots = jnp.zeros((EDGE, 2 * EDGE), jnp.float32)
        for k in range(EDGE):
            column = jnp.broadcast_to(state[:, k : k + 1], (EDGE, 2 * EDGE))
            pivot = column[k : k + 1, :]
            line = state[k : k + 1, :] / pivot
            pivots = jnp.where(rows == k, jnp.broadcast_to(pivot, rows.shape), pivots)
            if k < EDGE - 1:
                state = state - jnp.where(rows > k, column, 0.0) * line
        inverse = (state * lax.rsqrt(pivots))[:, EDGE:]
        upper = mm(inverse, work_ref[here, :], ((1,), (0,)))
        out_ref[here, :] = pltpu.roll(upper, i * EDGE, 1)[:, R:]
        rest = jnp.where(rest_lanes < (blocks - i) * EDGE, upper[:, :R], 0.0)
        change = mm(rest, upper, ((0,), (0,)))
        for r in range(1, blocks):
            there = pl.ds(pl.multiple_of(((i + r) % blocks) * EDGE, EDGE), EDGE)
            left = work_ref[there, :] - change[r * EDGE : (r + 1) * EDGE, :]
            work_ref[there, :] = pltpu.roll(left, 2 * R - EDGE, 1)
        return 0

    lax.fori_loop(0, blocks, step, 0)


def inverse_factor(gram):
    return pl.pallas_call(
        inverse_factor_kernel,
        out_shape=jax.ShapeDtypeStruct((R, R), jnp.float32),
        scratch_shapes=[pltpu.VMEM((R, 2 * R), jnp.float32)],
        cost_estimate=pl.CostEstimate(flops=10**8, transcendentals=0, bytes_accessed=6 * 10**7),
        name="inverse_factor",
    )(gram)


def product_kernel(place_ref, own_ref, *refs):
    outs, acts, (kept_ref, given_ref) = refs[: NX - 1], refs[NX - 1 : 2 * NX - 1], refs[2 * NX - 1 :]
    total = None
    for o_ref, a_ref in zip((own_ref, *outs), acts):
        part = lax.dot_general(
            o_ref[...].reshape(o_ref.shape[-2:]).astype(jnp.bfloat16),
            a_ref[...].astype(jnp.bfloat16),
            (((1,), (0,)), ((), ())),
            preferred_element_type=jnp.float32,
        )
        total = part if total is None else total + part
    near, far = total[: total.shape[0] // NC], total[total.shape[0] // NC :]
    first = place_ref[1] == 0
    kept_ref[...] = jnp.where(first, near, far)
    given_ref[...] = jnp.where(first, far, near)


def core_products(place, by_x, arrived, acts):
    block, tokens = by_x.shape[2:]
    cols = acts[0].shape[1]
    half = jax.ShapeDtypeStruct((NZ * block // NC, cols), jnp.float32)
    half_spec = pl.BlockSpec((block // NC, cols), lambda i, place: (i, 0))
    pair = NZ // NY

    def source(k):
        def index(i, place):
            return ((place[2] - i // pair) & (NY - 1), k - 1, i % pair, 0)

        return pl.BlockSpec((1, 1, block, tokens), index)

    return pl.pallas_call(
        product_kernel,
        out_shape=(half, half),
        grid_spec=pltpu.PrefetchScalarGridSpec(
            num_scalar_prefetch=1,
            grid=(NZ,),
            in_specs=[pl.BlockSpec((1, 1, block, tokens), lambda i, place: (i, place[0], 0, 0))]
            + [source(k) for k in range(1, NX)]
            + [pl.BlockSpec((tokens, cols), lambda i, place: (0, 0))] * NX,
            out_specs=(half_spec, half_spec),
        ),
        name="core_products",
    )(place, by_x, *[arrived] * (NX - 1), *acts)


def over_tp(v):
    total = v
    for k in (1, 2, 3):
        total = total + shifted(v, "tp", NY, k)
    return total


def block_at(v, index, length):
    return lax.dynamic_slice_in_dim(v, index * length, length, 0)


def summed_piece(v, beside=None):
    c, x = lax.axis_index("c"), lax.axis_index("x")
    half = v.shape[0] // NC
    v = block_at(v, c, half) + other_core(block_at(v, 1 - c, half))
    part = half // NX
    total = block_at(v, x, part)
    for k in (1, 2, 3):
        block = block_at(v, (x + k) & (NX - 1), part)
        total = total + shifted(block, "x", NX, k)
    if beside is not None:
        total, beside = lax.optimization_barrier((total, beside))
    pieces = total.reshape(NZ, part // NZ, v.shape[1])
    return jnp.sum(lax.all_to_all(pieces, "z", 0, 0, tiled=True), axis=0), beside


def whole_of(piece, beside=None):
    c, x = lax.axis_index("c"), lax.axis_index("x")
    copies = jnp.broadcast_to(piece[None], (NZ, *piece.shape))
    part = lax.all_to_all(copies, "z", 0, 0, tiled=True).reshape(-1, piece.shape[1])
    if beside is not None:
        part, beside = lax.optimization_barrier((part, beside))
    arrived = [part] + [shifted(part, "x", NX, k) for k in (1, 2, 3)]
    arrived = jnp.stack(arrived)
    half = jnp.concatenate(
        [lax.dynamic_index_in_dim(arrived, (x - s) & (NX - 1), 0, keepdims=False) for s in range(NX)]
    )
    other = other_core(half)
    whole = jnp.concatenate([jnp.where(c == 0, half, other), jnp.where(c == 0, other, half)])
    return whole, beside


def on_device(activations, out_grad, momentum, right_prev):
    z, x, c = lax.axis_index("z"), lax.axis_index("x"), lax.axis_index("c")
    t = lax.axis_index("tp")
    mine = (z * NX + x) * NC + c
    acts = activations.astype(jnp.float32)
    held = jnp.concatenate([acts, momentum])
    n_tokens, n_cols = acts.shape
    n_rows = momentum.shape[0]

    outs_t = out_grad.astype(jnp.float32).T
    quarter = block_at(outs_t, t, n_cols)
    place = (
        lax.broadcasted_iota(jnp.int32, (n_cols, n_rows), 0)
        == lax.broadcasted_iota(jnp.int32, (n_cols, n_rows), 1) + mine * n_rows - t * n_cols
    )
    spread = jnp.concatenate([quarter, place.astype(jnp.float32)], axis=1)

    first = dot(held, right_prev, ((1,), (0,)))
    first = over_tp(first)

    by_x = outs_t.reshape(NZ, NX, NC * n_rows, n_tokens)
    pair = NZ // NY
    outs_x = []
    for k in range(1, NX):
        start = (t * pair, (x + k) & (NX - 1), 0, 0)
        block = lax.dynamic_slice(by_x, start, (pair, 1, NC * n_rows, n_tokens))
        outs_x.append(shifted(block.reshape(-1, n_tokens), "x", NX, k))
    outs_x = jnp.stack(outs_x)
    outs_y = [outs_x] + [shifted(outs_x, "tp", NY, k) for k in range(1, NY)]
    acts_here = [acts] + [shifted(acts, "x", NX, k) for k in range(1, NX)]

    left_piece, _ = summed_piece(dot(spread, first, ((1,), (0,))))
    left_quarter, _ = whole_of(left_piece)
    seen = dot(spread, left_quarter, ((0,), (0,)))
    seen, outs_y, acts_here = lax.optimization_barrier((seen, outs_y, acts_here))
    second = over_tp(seen)

    place = jnp.stack([x, c, t]).astype(jnp.int32)
    kept, given = core_products(place, by_x, jnp.stack(outs_y), acts_here)
    near = kept + other_core(given)
    grad = lax.psum_scatter(near, "z", scatter_dimension=0, tiled=True)

    own_gram = dot(left_quarter, left_quarter, ((0,), (0,)))
    own_gram, second = lax.optimization_barrier((own_gram, second))
    gram = over_tp(own_gram)
    raw_piece, gram = summed_piece(dot(held, second, ((0,), (0,))), gram)
    raw, gram = whole_of(raw_piece, gram)
    inverse = inverse_factor(gram)
    basis = dot(second[n_tokens:], inverse, ((1,), (1,)))
    right = dot(raw, inverse, ((1,), (1,)))
    squares = over_tp(jnp.broadcast_to(jnp.sum(right * right, axis=0)[None], (8, R)))[:1]
    factor = lax.rsqrt(squares / D + 1e-06)
    buffer = momentum + grad
    new_momentum = buffer - (1.0 - momentum_decay) * dot(basis, right, ((1,), (1,)))
    update = math.sqrt(D / R) * dot(basis * factor, right, ((1,), (1,)))
    own = R // (NZ * NX * NC)
    right_owned = lax.dynamic_slice_in_dim(right * factor, mine * own, own, 1)
    return (new_momentum, update, right_owned)


def solution(mesh):
    finer = Mesh(mesh.devices.reshape(NZ, NX, NC, mesh.shape["tp"]), ("z", "x", "c", "tp"))
    in_specs = (P(FSDP, "tp"), P(FSDP, None), P(FSDP, "tp"), P("tp", None))
    out_specs = (P(FSDP, "tp"), P(FSDP, "tp"), P("tp", FSDP))
    return jax.shard_map(
        on_device, mesh=finer, in_specs=in_specs, out_specs=out_specs, check_vma=False
    )
```

```python
import math

import jax
import jax.numpy as jnp
from jax import lax
from jax.experimental import pallas as pl
from jax.experimental.pallas import tpu as pltpu
from jax.sharding import Mesh
from jax.sharding import PartitionSpec as P

D = 5120
R = 256
NZ, NX, NC, NY = 8, 4, 2, 4
FSDP = ("z", "x", "c")
TOKENS = 128
ROWS = D // (NZ * NX * NC)
COLS = D // NY
HALF = COLS // NC
PART = HALF // NX
PAIR = NZ // NY
EDGE = 32
STEP = 128
BLOCKS = R // EDGE
F32 = jnp.float32

momentum_decay = 0.95


def shape(*dims):
    return jax.ShapeDtypeStruct(dims, F32)


def shifted(v, axis, n, k):
    return lax.ppermute(v, axis, [(i, (i + k) % n) for i in range(n)])


def other_core(v):
    return lax.ppermute(v, "c", [(0, 1), (1, 0)])


def over_tp(v):
    total = v
    for k in range(1, NY):
        total = total + shifted(v, "tp", NY, k)
    return total


def plain(a, b, dims):
    return lax.dot_general(a, b, (dims, ((), ())), preferred_element_type=F32)


def full(a, b, dims):
    return lax.dot_general(
        a, b, (dims, ((), ())), precision=lax.Precision.HIGHEST, preferred_element_type=F32
    )


def split(v):
    one = v.astype(jnp.bfloat16)
    rest = v - one.astype(F32)
    two = rest.astype(jnp.bfloat16)
    three = (rest - two.astype(F32)).astype(jnp.bfloat16)
    return three, two, one


def narrow_times(a, parts, dims):
    total = None
    for part in parts:
        term = plain(a, part, dims)
        total = term if total is None else total + term
    return total


def call(kernel, scalars, out_shape, in_specs, *args, out_specs=None, grid=(1,), scratch=()):
    if out_specs is None:
        leaves = out_shape if isinstance(out_shape, tuple) else (out_shape,)
        specs = tuple(whole(s.shape) for s in leaves)
        out_specs = specs if isinstance(out_shape, tuple) else specs[0]
    return pl.pallas_call(
        kernel,
        out_shape=out_shape,
        grid_spec=pltpu.PrefetchScalarGridSpec(
            num_scalar_prefetch=1,
            grid=grid,
            in_specs=in_specs,
            out_specs=out_specs,
            scratch_shapes=scratch,
        ),
    )(scalars, *args)


def whole(dims):
    zeros = (0,) * len(dims)
    return pl.BlockSpec(tuple(dims), lambda i, at: zeros)


X, C, T, FIRST = range(4)


def first_kernel(at, acts, momentum, right, out):
    out[...] = jnp.zeros((TOKENS + ROWS, R), F32)

    def step(i, _):
        here = pl.ds(pl.multiple_of(i * 2 * STEP, STEP), 2 * STEP)
        block = right[here, :]
        out[:TOKENS, :] += narrow_times(acts[:, here], split(block), ((1,), (0,)))
        out[TOKENS:, :] += full(momentum[:, here], block, ((1,), (0,)))
        return 0

    lax.fori_loop(0, COLS // (2 * STEP), step, 0)


def turn_kernel(at, outs, out):
    out[...] = outs[...].astype(F32).T.reshape(NX, 1, NC * ROWS, TOKENS)


def left_kernel(at, near_outs, far_outs, v, kept, given):
    parts = split(v[:TOKENS, :])
    kept[...] = narrow_times(near_outs[...], parts, ((0,), (0,)))
    given[...] = narrow_times(far_outs[...], parts, ((0,), (0,)))
    first = at[FIRST]
    inside = (first >= 0) & (first < COLS)
    in_half = first // HALF
    for half, out in ((at[C], kept), (1 - at[C], given)):

        @pl.when(inside & (in_half == half))
        def _():
            here = pl.ds(pl.multiple_of(first - half * HALF, 8), ROWS)
            out[here, :] = out[here, :] + v[TOKENS:, :]


def seen_kernel(at, near_outs, far_outs, near, far, out):
    out[:TOKENS, :] = narrow_times(
        near_outs[...], split(near[...]), ((1,), (0,))
    ) + narrow_times(far_outs[...], split(far[...]), ((1,), (0,)))
    out[TOKENS:, :] = jnp.zeros((ROWS, R), F32)
    first = at[FIRST]
    inside = (first >= 0) & (first < COLS)
    in_half = first // HALF
    for half, source in ((at[C], near), (1 - at[C], far)):

        @pl.when(inside & (in_half == half))
        def _():
            here = pl.ds(pl.multiple_of(first - half * HALF, 8), ROWS)
            out[TOKENS:, :] = source[here, :]


def gram_kernel(at, near, far, out):
    out[...] = jnp.zeros((R, R), F32)

    def step(i, _):
        here = pl.ds(pl.multiple_of(i * STEP, STEP), STEP)
        block = jnp.concatenate([near[here, :], far[here, :]], axis=0)
        out[...] += full(block, block, ((0,), (0,)))
        return 0

    lax.fori_loop(0, HALF // STEP, step, 0)


def raw_kernel(at, near_acts, far_acts, near_mom, far_mom, v, kept, given):
    parts = split(v[:TOKENS, :])
    low = v[TOKENS:, :]

    def step(i, _):
        here = pl.ds(pl.multiple_of(i * STEP, STEP), STEP)
        for acts, mom, out in ((near_acts, near_mom, kept), (far_acts, far_mom, given)):
            top = narrow_times(acts[:, here], parts, ((0,), (0,)))
            out[here, :] = top + full(mom[:, here], low, ((0,), (0,)))
        return 0

    lax.fori_loop(0, HALF // STEP, step, 0)


def share_kernel(at, kept, arrived, *outs):
    for k, out in enumerate(outs):
        here = pl.ds(pl.multiple_of(((at[X] + k) & (NX - 1)) * PART, 8), PART)
        out[...] = kept[here, :] + arrived[here, :]


def gather_kernel(at, *refs):
    out = refs[-1]
    for k, ref in enumerate(refs[:-1]):
        here = pl.ds(pl.multiple_of(((at[X] - k) & (NX - 1)) * PART, 8), PART)
        out[here, :] = ref[...]


def right_kernel(at, near, far, inverse, out, squares):
    n = inverse[...]

    def step(i, total):
        here = pl.ds(pl.multiple_of(i * STEP, STEP), STEP)
        block = jnp.concatenate([near[here, :], far[here, :]], axis=0)
        value = full(block, n, ((1,), (1,)))
        for k, half in enumerate((at[C], 1 - at[C])):
            there = pl.ds(pl.multiple_of(half * HALF + i * STEP, STEP), STEP)
            out[there, :] = value[k * STEP : (k + 1) * STEP, :]
        return total + jnp.sum(value * value, axis=0, keepdims=True)

    total = lax.fori_loop(0, HALF // STEP, step, jnp.zeros((1, R), F32))
    squares[...] = jnp.broadcast_to(total, (8, R))


def update_kernel(at, basis, right, factor, change, update):
    left = jnp.concatenate([basis[...], basis[...] * factor[:1, :]], axis=0)

    def step(i, _):
        here = pl.ds(pl.multiple_of(i * 2 * STEP, STEP), 2 * STEP)
        value = full(left, right[here, :], ((1,), (1,)))
        change[:, here] = (1.0 - momentum_decay) * value[:ROWS, :]
        update[:, here] = math.sqrt(D / R) * value[ROWS:, :]
        return 0

    lax.fori_loop(0, COLS // (2 * STEP), step, 0)


def eliminate(first_block, count, work_ref, out_ref):
    rows = lax.broadcasted_iota(jnp.int32, (EDGE, 2 * EDGE), 0)
    lanes = lax.broadcasted_iota(jnp.int32, (EDGE, 2 * EDGE), 1)
    eye = (rows + EDGE == lanes).astype(F32)
    rest_lanes = lax.broadcasted_iota(jnp.int32, (EDGE, R), 1)

    def step(i, _):
        here = pl.ds(pl.multiple_of(i * EDGE, EDGE), EDGE)
        state = jnp.where(lanes < EDGE, work_ref[here, : 2 * EDGE], eye)
        pivots = jnp.zeros((EDGE, 2 * EDGE), F32)
        for k in range(EDGE):
            column = jnp.broadcast_to(state[:, k : k + 1], (EDGE, 2 * EDGE))
            pivot = column[k : k + 1, :]
            line = state[k : k + 1, :] / pivot
            pivots = jnp.where(rows == k, jnp.broadcast_to(pivot, rows.shape), pivots)
            if k < EDGE - 1:
                state = state - jnp.where(rows > k, column, 0.0) * line
        inverse = (state * lax.rsqrt(pivots))[:, EDGE:]
        upper = full(inverse, work_ref[here, :], ((1,), (0,)))
        out_ref[here, :] = pltpu.roll(upper, i * EDGE, 1)[:, R:]
        rest = jnp.where(rest_lanes < (BLOCKS - i) * EDGE, upper[:, :R], 0.0)
        change = full(rest, upper, ((0,), (0,)))
        for r in range(1, BLOCKS):
            there = pl.ds(pl.multiple_of(((i + r) % BLOCKS) * EDGE, EDGE), EDGE)
            left = work_ref[there, :] - change[r * EDGE : (r + 1) * EDGE, :]
            work_ref[there, :] = pltpu.roll(left, 2 * R - EDGE, 1)
        return 0

    lax.fori_loop(first_block, first_block + count, step, 0)


def early_kernel(at, gram, work, out):
    all_rows = lax.broadcasted_iota(jnp.int32, (R, R), 0)
    all_lanes = lax.broadcasted_iota(jnp.int32, (R, R), 1)
    work[:, :R] = gram[...]
    work[:, R:] = (all_rows == all_lanes).astype(F32)
    out[...] = jnp.zeros((R, R), F32)
    eliminate(0, BLOCKS // 2, work, out)


def late_kernel(at, work, done, out, held):
    held[...] = work[...]
    out[...] = done[...]
    eliminate(BLOCKS // 2, BLOCKS // 2, held, out)


def product_kernel(at, outs, acts, kept, given, joined):
    @pl.when(pl.program_id(0) == 0)
    def _():
        joined[...] = acts[...].astype(jnp.bfloat16)

    lhs = jnp.concatenate([outs[0, k].astype(jnp.bfloat16) for k in range(NX)], axis=1)
    total = plain(lhs, joined[...], ((1,), (0,)))
    first = at[C] == 0
    for i in range(PAIR):
        near = total[NC * i * ROWS : (NC * i + 1) * ROWS]
        far = total[(NC * i + 1) * ROWS : (NC * i + 2) * ROWS]
        kept[i * ROWS : (i + 1) * ROWS, :] = jnp.where(first, near, far)
        given[i * ROWS : (i + 1) * ROWS, :] = jnp.where(first, far, near)


def core_products(at, outs, acts):
    half = shape(NZ * ROWS, COLS)
    half_spec = pl.BlockSpec((PAIR * ROWS, COLS), lambda i, at: (i, 0))
    outs_spec = pl.BlockSpec((1, NX, PAIR * NC * ROWS, TOKENS), lambda i, at: (i, 0, 0, 0))
    return call(
        product_kernel, at, (half, half), [outs_spec, whole(acts.shape)],
        outs, acts, out_specs=(half_spec, half_spec), grid=(NY,),
        scratch=[pltpu.VMEM(acts.shape, jnp.bfloat16)],
    )


def half_blocks(rows, quarter):
    scale = NC if quarter else 0
    near = pl.BlockSpec((rows, HALF), lambda i, at: (0, scale * at[T] + at[C]))
    far = pl.BlockSpec((rows, HALF), lambda i, at: (0, scale * at[T] + 1 - at[C]))
    return [near, far]


def summed_piece(at, kept, given, beside=None):
    arrived = other_core(given)
    blocks = call(share_kernel, at, (shape(PART, R),) * NX, [whole((HALF, R))] * 2, kept, arrived)
    total = blocks[0]
    for k in range(1, NX):
        total = total + shifted(blocks[k], "x", NX, k)
    if beside is not None:
        total, beside = lax.optimization_barrier((total, beside))
    pieces = total.reshape(NZ, PART // NZ, R)
    arrived = lax.all_to_all(pieces, "z", 0, 0, tiled=True)
    return jnp.sum(arrived, axis=0), beside


def whole_of(at, piece):
    copies = jnp.broadcast_to(piece[None], (NZ, *piece.shape))
    part = lax.all_to_all(copies, "z", 0, 0, tiled=True)
    part = part.reshape(PART, R)
    arrived = [part] + [shifted(part, "x", NX, k) for k in range(1, NX)]
    near = call(gather_kernel, at, shape(HALF, R), [whole((PART, R))] * NX, *arrived)
    return near, other_core(near)


def on_device(activations, out_grad, momentum, right_prev):
    z, x, c = lax.axis_index("z"), lax.axis_index("x"), lax.axis_index("c")
    t = lax.axis_index("tp")
    mine = (z * NX + x) * NC + c
    at = jnp.stack([x, c, t, mine * ROWS - t * COLS]).astype(jnp.int32)
    outs_halves, acts_halves = half_blocks(TOKENS, True), half_blocks(TOKENS, False)
    mom_halves = half_blocks(ROWS, False)
    two_halves = (shape(HALF, R),) * 2
    tall = shape(TOKENS + ROWS, R)

    first = call(
        first_kernel, at, tall,
        [whole((TOKENS, COLS)), whole((ROWS, COLS)), whole((COLS, R))],
        activations, momentum, right_prev,
    )
    first = over_tp(first)

    acts = lax.all_gather(activations.astype(F32), "x", axis=0, tiled=True)
    turned = call(
        turn_kernel, at, shape(NX, PAIR, NC * ROWS, TOKENS),
        [pl.BlockSpec((TOKENS, D // NZ), lambda i, at: (0, PAIR * at[T] + i))], out_grad,
        out_specs=pl.BlockSpec((NX, 1, NC * ROWS, TOKENS), lambda i, at: (0, i, 0, 0)),
        grid=(PAIR,),
    )
    turned = turned.reshape(NX, PAIR * NC * ROWS, TOKENS)
    outs = lax.all_to_all(turned, "x", 0, 0, tiled=True)
    outs = lax.all_gather(outs, "tp", axis=0, tiled=False)

    kept, given = call(
        left_kernel, at, two_halves, [*outs_halves, whole(tall.shape)],
        out_grad, out_grad, first,
    )
    piece, _ = summed_piece(at, kept, given)
    near, far = whole_of(at, piece)
    seen = call(
        seen_kernel, at, tall, [*outs_halves, whole((HALF, R)), whole((HALF, R))],
        out_grad, out_grad, near, far,
    )
    seen, at_seen = lax.optimization_barrier((seen, at))
    second = over_tp(seen)

    kept_grad, given_grad = core_products(at_seen, outs, acts)
    gram = call(gram_kernel, at, shape(R, R), [whole((HALF, R))] * 2, near, far)
    kept_grad, gram, second = lax.optimization_barrier((kept_grad, gram, second))
    summed_grad = kept_grad + other_core(given_grad)
    grad = lax.psum_scatter(summed_grad, "z", scatter_dimension=0, tiled=True)
    gram = over_tp(gram)

    kept, given = call(
        raw_kernel, at, two_halves, [*acts_halves, *mom_halves, whole(tall.shape)],
        activations, activations, momentum, momentum, second,
    )
    piece, gram = summed_piece(at, kept, given, gram)
    work, done = call(early_kernel, at, (shape(R, 2 * R), shape(R, R)), [whole((R, R))], gram)
    piece, work = lax.optimization_barrier((piece, work))
    near, far = whole_of(at, piece)
    inverse = call(
        late_kernel, at, shape(R, R), [whole((R, 2 * R)), whole((R, R))], work, done,
        scratch=[pltpu.VMEM((R, 2 * R), F32)],
    )
    basis = lax.dot_general(
        second[TOKENS:], inverse, (((1,), (1,)), ((), ())), precision=lax.Precision.HIGHEST
    )
    right, squares = call(
        right_kernel, at, (shape(COLS, R), shape(8, R)),
        [whole((HALF, R)), whole((HALF, R)), whole((R, R))], near, far, inverse,
    )
    squares = over_tp(squares)
    factor = lax.rsqrt(squares / D + 1e-06)
    change, update = call(
        update_kernel, at, (shape(ROWS, COLS),) * 2,
        [whole((ROWS, R)), whole((COLS, R)), whole((8, R))], basis, right, factor,
    )
    new_momentum = (momentum + grad) - change
    own = R // (NZ * NX * NC)
    right_owned = lax.dynamic_slice_in_dim(right, mine * own, own, 1)
    right_owned = right_owned * lax.dynamic_slice_in_dim(factor[:1], mine * own, own, 1)
    return (new_momentum, update, right_owned)


def solution(mesh):
    finer = Mesh(mesh.devices.reshape(NZ, NX, NC, mesh.shape["tp"]), ("z", "x", "c", "tp"))
    in_specs = (P(FSDP, "tp"), P(FSDP, None), P(FSDP, "tp"), P("tp", None))
    out_specs = (P(FSDP, "tp"), P(FSDP, "tp"), P("tp", FSDP))
    return jax.shard_map(
        on_device, mesh=finer, in_specs=in_specs, out_specs=out_specs, check_vma=False
    )
```

```python
import math

import jax
import jax.numpy as jnp
from jax import lax
from jax.experimental import pallas as pl
from jax.experimental.pallas import tpu as pltpu
from jax.sharding import Mesh
from jax.sharding import PartitionSpec as P

D = 5120
R = 256
NZ, NX, NC, NY = 8, 4, 2, 4
FSDP = ("z", "x", "c")
TOKENS = 128
ROWS = D // (NZ * NX * NC)
COLS = D // NY
HALF = COLS // NC
PAIR = NZ // NY
EDGE = 64
BLOCKS = R // EDGE
F32 = jnp.float32

momentum_decay = 0.95


def shape(*dims):
    return jax.ShapeDtypeStruct(dims, F32)


def shifted(v, axis, n, k):
    return lax.ppermute(v, axis, [(i, (i + k) % n) for i in range(n)])


def other_core(v):
    return lax.ppermute(v, "c", [(0, 1), (1, 0)])


def over_tp(v):
    total = v
    for k in range(1, NY):
        total = total + shifted(v, "tp", NY, k)
    return total


def plain(a, b, dims):
    return lax.dot_general(a, b, (dims, ((), ())), preferred_element_type=F32)


def full(a, b, dims):
    return lax.dot_general(
        a, b, (dims, ((), ())), precision=lax.Precision.HIGHEST, preferred_element_type=F32
    )


def near_dot(a, b, dims):
    return lax.dot_general(
        a, b, (dims, ((), ())), precision=lax.Precision.HIGH, preferred_element_type=F32
    )


def call(kernel, scalars, out_shape, in_specs, *args, out_specs=None, grid=(1,), scratch=()):
    if out_specs is None:
        leaves = out_shape if isinstance(out_shape, tuple) else (out_shape,)
        specs = tuple(whole(s.shape) for s in leaves)
        out_specs = specs if isinstance(out_shape, tuple) else specs[0]
    return pl.pallas_call(
        kernel,
        out_shape=out_shape,
        grid_spec=pltpu.PrefetchScalarGridSpec(
            num_scalar_prefetch=1,
            grid=grid,
            in_specs=in_specs,
            out_specs=out_specs,
            scratch_shapes=scratch,
        ),
    )(scalars, *args)


def whole(dims):
    zeros = (0,) * len(dims)
    return pl.BlockSpec(tuple(dims), lambda i, at: zeros)


C, T = range(2)


def turn_kernel(at, outs, out):
    out[...] = outs[...].astype(F32).T.reshape(NX, 1, NC * ROWS, TOKENS)


def eliminate(first_block, count, work_ref, out_ref):
    rows = lax.broadcasted_iota(jnp.int32, (EDGE, 2 * EDGE), 0)
    lanes = lax.broadcasted_iota(jnp.int32, (EDGE, 2 * EDGE), 1)
    eye = (rows + EDGE == lanes).astype(F32)
    rest_lanes = lax.broadcasted_iota(jnp.int32, (EDGE, R), 1)

    def step(i, _):
        here = pl.ds(pl.multiple_of(i * EDGE, EDGE), EDGE)
        state = jnp.where(lanes < EDGE, work_ref[here, : 2 * EDGE], eye)
        pivots = jnp.zeros((EDGE, 2 * EDGE), F32)
        for k in range(EDGE):
            column = jnp.broadcast_to(state[:, k : k + 1], (EDGE, 2 * EDGE))
            pivot = column[k : k + 1, :]
            line = state[k : k + 1, :] / pivot
            pivots = jnp.where(rows == k, jnp.broadcast_to(pivot, rows.shape), pivots)
            if k < EDGE - 1:
                state = state - jnp.where(rows > k, column, 0.0) * line
        inverse = (state * lax.rsqrt(pivots))[:, EDGE:]
        upper = full(inverse, work_ref[here, :], ((1,), (0,)))
        out_ref[here, :] = pltpu.roll(upper, i * EDGE, 1)[:, R:]
        rest = jnp.where(rest_lanes < (BLOCKS - i) * EDGE, upper[:, :R], 0.0)
        change = full(rest, upper, ((0,), (0,)))
        for r in range(1, BLOCKS):
            there = pl.ds(pl.multiple_of(((i + r) % BLOCKS) * EDGE, EDGE), EDGE)
            left = work_ref[there, :] - change[r * EDGE : (r + 1) * EDGE, :]
            work_ref[there, :] = pltpu.roll(left, 2 * R - EDGE, 1)
        return 0

    lax.fori_loop(first_block, first_block + count, step, 0)


def early_kernel(at, gram, work, out):
    all_rows = lax.broadcasted_iota(jnp.int32, (R, R), 0)
    all_lanes = lax.broadcasted_iota(jnp.int32, (R, R), 1)
    work[:, :R] = gram[...]
    work[:, R:] = (all_rows == all_lanes).astype(F32)
    out[...] = jnp.zeros((R, R), F32)
    eliminate(0, BLOCKS // 2, work, out)


def late_kernel(at, work, done, out, held):
    held[...] = work[...]
    out[...] = done[...]
    eliminate(BLOCKS // 2, BLOCKS // 2, held, out)


def product_kernel(at, outs, acts, kept, given, joined):
    @pl.when(pl.program_id(0) == 0)
    def _():
        joined[...] = acts[...].astype(jnp.bfloat16)

    lhs = jnp.concatenate([outs[0, k].astype(jnp.bfloat16) for k in range(NX)], axis=1)
    total = plain(lhs, joined[...], ((1,), (0,)))
    first = at[C] == 0
    for i in range(PAIR):
        near = total[NC * i * ROWS : (NC * i + 1) * ROWS]
        far = total[(NC * i + 1) * ROWS : (NC * i + 2) * ROWS]
        kept[i * ROWS : (i + 1) * ROWS, :] = jnp.where(first, near, far)
        given[i * ROWS : (i + 1) * ROWS, :] = jnp.where(first, far, near)


def core_products(at, outs, acts):
    half = shape(NZ * ROWS, COLS)
    half_spec = pl.BlockSpec((PAIR * ROWS, COLS), lambda i, at: (i, 0))
    outs_spec = pl.BlockSpec((1, NX, PAIR * NC * ROWS, TOKENS), lambda i, at: (i, 0, 0, 0))
    return call(
        product_kernel, at, (half, half), [outs_spec, whole(acts.shape)],
        outs, acts, out_specs=(half_spec, half_spec), grid=(NY,),
        scratch=[pltpu.VMEM(acts.shape, jnp.bfloat16)],
    )


def summed_piece(kept, given):
    pieces = (kept + other_core(given)).reshape(NX * NZ, HALF // (NX * NZ), R)
    arrived = lax.all_to_all(pieces, ("x", "z"), 0, 0, tiled=True)
    return jnp.sum(arrived, axis=0)


def spread_over(v, axis, n):
    copies = jnp.broadcast_to(v[None], (n, *v.shape))
    return lax.all_to_all(copies, axis, 0, 0, tiled=True).reshape(-1, v.shape[1])


def gathered(piece):
    part = spread_over(piece, "z", NZ)
    near = spread_over(part, "x", NX)
    return near, other_core(near)


def on_device(activations, out_grad, momentum, right_prev):
    z, x, c = lax.axis_index("z"), lax.axis_index("x"), lax.axis_index("c")
    t = lax.axis_index("tp")
    mine = (z * NX + x) * NC + c
    at = jnp.stack([c, t]).astype(jnp.int32)

    held = jnp.concatenate([activations.astype(F32), momentum])
    first = near_dot(held, right_prev, ((1,), (0,)))
    first, activations, out_grad = lax.optimization_barrier((first, activations, out_grad))
    first = over_tp(first)

    acts = lax.all_gather(activations.astype(F32), "x", axis=0, tiled=True)
    turned = call(
        turn_kernel, at, shape(NX, PAIR, NC * ROWS, TOKENS),
        [pl.BlockSpec((TOKENS, D // NZ), lambda i, at: (0, PAIR * at[T] + i))], out_grad,
        out_specs=pl.BlockSpec((NX, 1, NC * ROWS, TOKENS), lambda i, at: (0, i, 0, 0)),
        grid=(PAIR,),
    )
    turned = turned.reshape(NX, PAIR * NC * ROWS, TOKENS)
    outs = lax.all_to_all(turned, "x", 0, 0, tiled=True)
    outs = lax.all_gather(outs, "tp", axis=0, tiled=False)

    helds, spreads = [], []
    for half in (c, 1 - c):
        helds.append(lax.dynamic_slice_in_dim(held, half * HALF, HALF, 1))
        start = t * COLS + half * HALF
        place = lax.broadcasted_iota(jnp.int32, (ROWS, HALF), 0) + (mine * ROWS - start)
        place = place == lax.broadcasted_iota(jnp.int32, (ROWS, HALF), 1)
        part = lax.dynamic_slice_in_dim(out_grad, start, HALF, 1)
        spreads.append(jnp.concatenate([part.astype(F32), place.astype(F32)]))

    given = near_dot(spreads[1], first, ((0,), (0,)))
    kept = near_dot(spreads[0], first, ((0,), (0,)))
    piece = summed_piece(kept, given)
    near, far = gathered(piece)
    seen = near_dot(spreads[0], near, ((1,), (0,))) + near_dot(spreads[1], far, ((1,), (0,)))
    second = over_tp(seen)

    gram = full(near, near, ((0,), (0,))) + full(far, far, ((0,), (0,)))
    gram, second = lax.optimization_barrier((gram, second))
    gram = over_tp(gram)

    given = near_dot(helds[1], second, ((0,), (0,)))
    kept = near_dot(helds[0], second, ((0,), (0,)))
    given, at_right = lax.optimization_barrier((given, at))
    piece = summed_piece(kept, given)
    kept_grad, given_grad = core_products(at_right, outs, acts)
    summed_grad = kept_grad + other_core(given_grad)
    grad = lax.psum_scatter(summed_grad, "z", scatter_dimension=0, tiled=True)
    work, done = call(early_kernel, at, (shape(R, 2 * R), shape(R, R)), [whole((R, R))], gram)
    near, far = gathered(piece)
    inverse = call(
        late_kernel, at, shape(R, R), [whole((R, 2 * R)), whole((R, R))], work, done,
        scratch=[pltpu.VMEM((R, 2 * R), F32)],
    )
    basis = near_dot(second[TOKENS:], inverse, ((1,), (1,)))
    rights = [near_dot(v, inverse, ((1,), (1,))) for v in (near, far)]
    squares = sum(jnp.sum(v * v, axis=0) for v in rights)
    squares = over_tp(jnp.broadcast_to(squares[None], (8, R)))[:1]
    factor = lax.rsqrt(squares / D + 1e-06)

    def in_order(pair, axis):
        return jnp.concatenate(
            [jnp.where(c == 0, pair[0], pair[1]), jnp.where(c == 0, pair[1], pair[0])], axis=axis
        )

    change = in_order([near_dot(basis, v, ((1,), (1,))) for v in rights], 1)
    update = in_order([near_dot(basis * factor, v, ((1,), (1,))) for v in rights], 1)
    new_momentum = (momentum + grad) - (1.0 - momentum_decay) * change
    own = R // (NZ * NX * NC)
    owned = in_order([lax.dynamic_slice_in_dim(v, mine * own, own, 1) for v in rights], 0)
    owned = owned * lax.dynamic_slice_in_dim(factor, mine * own, own, 1)
    return (new_momentum, math.sqrt(D / R) * update, owned)


def solution(mesh):
    finer = Mesh(mesh.devices.reshape(NZ, NX, NC, mesh.shape["tp"]), ("z", "x", "c", "tp"))
    in_specs = (P(FSDP, "tp"), P(FSDP, None), P(FSDP, "tp"), P("tp", None))
    out_specs = (P(FSDP, "tp"), P(FSDP, "tp"), P("tp", FSDP))
    return jax.shard_map(
        on_device, mesh=finer, in_specs=in_specs, out_specs=out_specs, check_vma=False
    )
```

```python
import math

import jax
import jax.numpy as jnp
from jax import lax
from jax.experimental import pallas as pl
from jax.experimental.pallas import tpu as pltpu
from jax.sharding import Mesh
from jax.sharding import PartitionSpec as P

D = 5120
R = 256
NZ, NX, NC, NY = 8, 4, 2, 4
FSDP = ("z", "x", "c")
TOKENS = 128
ROWS = D // (NZ * NX * NC)
COLS = D // NY
HALF = COLS // NC
PAIR = NZ // NY
STEP = 128
EDGE = 64
GROUP = 8
BLOCKS = R // EDGE
F32 = jnp.float32

momentum_decay = 0.95


def shape(*dims):
    return jax.ShapeDtypeStruct(dims, F32)


def shifted(v, axis, n, k):
    return lax.ppermute(v, axis, [(i, (i + k) % n) for i in range(n)])


def other_core(v):
    return lax.ppermute(v, "c", [(0, 1), (1, 0)])


def over_tp(v):
    total = v
    for k in range(1, NY):
        total = total + shifted(v, "tp", NY, k)
    return total


def plain(a, b, dims):
    return lax.dot_general(a, b, (dims, ((), ())), preferred_element_type=F32)


def full(a, b, dims):
    return lax.dot_general(
        a, b, (dims, ((), ())), precision=lax.Precision.HIGHEST, preferred_element_type=F32
    )


def near_dot(a, b, dims):
    return lax.dot_general(
        a, b, (dims, ((), ())), precision=lax.Precision.HIGH, preferred_element_type=F32
    )


def call(kernel, scalars, out_shape, in_specs, *args, out_specs=None, grid=(1,), scratch=()):
    if out_specs is None:
        leaves = out_shape if isinstance(out_shape, tuple) else (out_shape,)
        specs = tuple(whole(s.shape) for s in leaves)
        out_specs = specs if isinstance(out_shape, tuple) else specs[0]
    return pl.pallas_call(
        kernel,
        out_shape=out_shape,
        grid_spec=pltpu.PrefetchScalarGridSpec(
            num_scalar_prefetch=1,
            grid=grid,
            in_specs=in_specs,
            out_specs=out_specs,
            scratch_shapes=scratch,
        ),
    )(scalars, *args)


def whole(dims):
    zeros = (0,) * len(dims)
    return pl.BlockSpec(tuple(dims), lambda i, at: zeros)


C, T, X = range(3)


def gram_kernel(at, near, far, out):
    out[...] = jnp.zeros((R, R), F32)

    def step(i, _):
        here = pl.ds(pl.multiple_of(i * STEP, STEP), STEP)
        block = jnp.concatenate([near[here, :], far[here, :]], axis=0)
        out[...] += full(block, block, ((0,), (0,)))
        return 0

    lax.fori_loop(0, HALF // STEP, step, 0)


def turn_kernel(at, outs, out):
    out[...] = outs[...].astype(F32).T.reshape(NX, 1, NC * ROWS, TOKENS)


def factor_kernel(at, work_in, done, work_ref, out_ref):
    work_ref[...] = work_in[...]
    out_ref[...] = done[...]
    rows = lax.broadcasted_iota(jnp.int32, (EDGE, 2 * EDGE), 0)
    lanes = lax.broadcasted_iota(jnp.int32, (EDGE, 2 * EDGE), 1)
    eye = (rows + EDGE == lanes).astype(F32)
    rest_lanes = lax.broadcasted_iota(jnp.int32, (EDGE, R), 1)

    def step(j, _):
        i = at[0] + j
        here = pl.ds(pl.multiple_of(i * EDGE, EDGE), EDGE)
        state = jnp.where(lanes < EDGE, work_ref[here, : 2 * EDGE], eye)
        pivots = jnp.zeros((EDGE, 2 * EDGE), F32)

        def group(g, carry):
            state, pivots = carry
            live = rows < EDGE - GROUP * g
            for k in range(GROUP):
                column = jnp.broadcast_to(state[:, k : k + 1], (EDGE, 2 * EDGE))
                pivot = column[k : k + 1, :]
                line = state[k : k + 1, :] / pivot
                pivots = jnp.where(rows == k, jnp.broadcast_to(pivot, rows.shape), pivots)
                state = state - jnp.where((rows > k) & live, column, 0.0) * line
            state = jnp.concatenate([state[GROUP:], state[:GROUP]], axis=0)
            pivots = jnp.concatenate([pivots[GROUP:], pivots[:GROUP]], axis=0)
            return pltpu.roll(state, 2 * EDGE - GROUP, 1), pivots

        state, pivots = lax.fori_loop(0, EDGE // GROUP, group, (state, pivots))
        inverse = (state * lax.rsqrt(pivots))[:, :EDGE]
        upper = full(inverse, work_ref[here, :], ((1,), (0,)))
        out_ref[here, :] = pltpu.roll(upper, i * EDGE, 1)[:, R:]
        rest = jnp.where(rest_lanes < (BLOCKS - i) * EDGE, upper[:, :R], 0.0)
        change = full(rest, upper, ((0,), (0,)))
        for r in range(1, BLOCKS):
            there = pl.ds(pl.multiple_of(((i + r) % BLOCKS) * EDGE, EDGE), EDGE)
            left = work_ref[there, :] - change[r * EDGE : (r + 1) * EDGE, :]
            work_ref[there, :] = pltpu.roll(left, 2 * R - EDGE, 1)
        return 0

    lax.fori_loop(0, BLOCKS // 2, step, 0)


def factor_step(first_block, work, done):
    return call(
        factor_kernel, jnp.full((1,), first_block, jnp.int32),
        (shape(R, 2 * R), shape(R, R)), [whole((R, 2 * R)), whole((R, R))], work, done,
    )


def product_kernel(at, *refs):
    sources, (acts, kept, given, joined, lhs) = refs[:NY], refs[NY:]

    @pl.when(pl.program_id(0) == 0)
    def _():
        for k in range(NX):
            here = pl.ds(pl.multiple_of(((at[X] - k) & (NX - 1)) * TOKENS, TOKENS), TOKENS)
            joined[k * TOKENS : (k + 1) * TOKENS, :] = acts[here, :].astype(jnp.bfloat16)

    for j, source in enumerate(sources):

        @pl.when(((at[T] - pl.program_id(0)) & (NY - 1)) == j)
        def _():
            for k in range(NX):
                lhs[:, k * TOKENS : (k + 1) * TOKENS] = source[k].astype(jnp.bfloat16)

    total = plain(lhs[...], joined[...], ((1,), (0,)))
    first = at[C] == 0
    for i in range(PAIR):
        near = total[NC * i * ROWS : (NC * i + 1) * ROWS]
        far = total[(NC * i + 1) * ROWS : (NC * i + 2) * ROWS]
        kept[i * ROWS : (i + 1) * ROWS, :] = jnp.where(first, near, far)
        given[i * ROWS : (i + 1) * ROWS, :] = jnp.where(first, far, near)


def core_products(at, outs, acts):
    half = shape(NZ * ROWS, COLS)
    half_spec = pl.BlockSpec((PAIR * ROWS, COLS), lambda i, at: (i, 0))
    return call(
        product_kernel, at, (half, half),
        [whole(v.shape) for v in outs] + [whole(acts.shape)], *outs, acts,
        out_specs=(half_spec, half_spec), grid=(NY,),
        scratch=[
            pltpu.VMEM(acts.shape, jnp.bfloat16),
            pltpu.VMEM((PAIR * NC * ROWS, NX * TOKENS), jnp.bfloat16),
        ],
    )


def summed_piece(kept, given):
    pieces = (kept + other_core(given)).reshape(NX * NZ, HALF // (NX * NZ), R)
    arrived = lax.all_to_all(pieces, ("x", "z"), 0, 0, tiled=True)
    return jnp.sum(arrived, axis=0)


def spread_over(v, axis, n):
    copies = jnp.broadcast_to(v[None], (n, *v.shape))
    return lax.all_to_all(copies, axis, 0, 0, tiled=True).reshape(-1, v.shape[1])


def gathered(piece):
    part = spread_over(piece, "z", NZ)
    near = spread_over(part, "x", NX)
    return near, other_core(near)


def on_device(activations, out_grad, momentum, right_prev):
    z, x, c = lax.axis_index("z"), lax.axis_index("x"), lax.axis_index("c")
    t = lax.axis_index("tp")
    mine = (z * NX + x) * NC + c
    at = jnp.stack([c, t, x]).astype(jnp.int32)

    held = jnp.concatenate([activations.astype(F32), momentum])
    first = near_dot(held, right_prev, ((1,), (0,)))
    first, activations, out_grad = lax.optimization_barrier((first, activations, out_grad))
    first = over_tp(first)

    acts = lax.all_gather(activations.astype(F32), "x", axis=0, tiled=True)
    turned = call(
        turn_kernel, at, shape(NX, PAIR, NC * ROWS, TOKENS),
        [pl.BlockSpec((TOKENS, D // NZ), lambda i, at: (0, PAIR * at[T] + i))], out_grad,
        out_specs=pl.BlockSpec((NX, 1, NC * ROWS, TOKENS), lambda i, at: (0, i, 0, 0)),
        grid=(PAIR,),
    )
    turned = turned.reshape(NX, PAIR * NC * ROWS, TOKENS)
    outs = []
    for k in range(NX):
        block = lax.dynamic_index_in_dim(turned, (x + k) & (NX - 1), 0, keepdims=False)
        outs.append(shifted(block, "x", NX, k) if k else block)
    outs = jnp.stack(outs)
    outs = [outs] + [shifted(outs, "tp", NY, k) for k in range(1, NY)]

    helds, spreads = [], []
    for half in (c, 1 - c):
        helds.append(lax.dynamic_slice_in_dim(held, half * HALF, HALF, 1))
        start = t * COLS + half * HALF
        place = lax.broadcasted_iota(jnp.int32, (ROWS, HALF), 0) + (mine * ROWS - start)
        place = place == lax.broadcasted_iota(jnp.int32, (ROWS, HALF), 1)
        part = lax.dynamic_slice_in_dim(out_grad, start, HALF, 1)
        spreads.append(jnp.concatenate([part.astype(F32), place.astype(F32)]))

    given = near_dot(spreads[1], first, ((0,), (0,)))
    kept = near_dot(spreads[0], first, ((0,), (0,)))
    piece = summed_piece(kept, given)
    piece, at_left = lax.optimization_barrier((piece, at))
    kept_grad, given_grad = core_products(at_left, outs, acts)
    near, far = gathered(piece)
    summed_grad = kept_grad + other_core(given_grad)
    grad = lax.psum_scatter(summed_grad, "z", scatter_dimension=0, tiled=True)
    seen = near_dot(spreads[0], near, ((1,), (0,))) + near_dot(spreads[1], far, ((1,), (0,)))
    second = over_tp(seen)

    gram = call(gram_kernel, at, shape(R, R), [whole((HALF, R))] * 2, near, far)
    gram, second = lax.optimization_barrier((gram, second))
    gram = over_tp(gram)

    given = near_dot(helds[1], second, ((0,), (0,)))
    kept = near_dot(helds[0], second, ((0,), (0,)))
    piece = summed_piece(kept, given)
    work = jnp.concatenate([gram, jnp.eye(R, dtype=F32)], axis=1)
    work, done = factor_step(0, work, jnp.zeros((R, R), F32))
    near, far = gathered(piece)
    _, inverse = factor_step(BLOCKS // 2, work, done)
    basis = near_dot(second[TOKENS:], inverse, ((1,), (1,)))
    rights = [near_dot(v, inverse, ((1,), (1,))) for v in (near, far)]
    squares = sum(jnp.sum(v * v, axis=0) for v in rights)
    squares = over_tp(jnp.broadcast_to(squares[None], (8, R)))[:1]
    factor = lax.rsqrt(squares / D + 1e-06)

    def in_order(pair, axis):
        return jnp.concatenate(
            [jnp.where(c == 0, pair[0], pair[1]), jnp.where(c == 0, pair[1], pair[0])], axis=axis
        )

    change = in_order([near_dot(basis, v, ((1,), (1,))) for v in rights], 1)
    update = in_order([near_dot(basis * factor, v, ((1,), (1,))) for v in rights], 1)
    new_momentum = (momentum + grad) - (1.0 - momentum_decay) * change
    own = R // (NZ * NX * NC)
    owned = in_order([lax.dynamic_slice_in_dim(v, mine * own, own, 1) for v in rights], 0)
    owned = owned * lax.dynamic_slice_in_dim(factor, mine * own, own, 1)
    return (new_momentum, math.sqrt(D / R) * update, owned)


def solution(mesh):
    finer = Mesh(mesh.devices.reshape(NZ, NX, NC, mesh.shape["tp"]), ("z", "x", "c", "tp"))
    in_specs = (P(FSDP, "tp"), P(FSDP, None), P(FSDP, "tp"), P("tp", None))
    out_specs = (P(FSDP, "tp"), P(FSDP, "tp"), P("tp", FSDP))
    return jax.shard_map(
        on_device, mesh=finer, in_specs=in_specs, out_specs=out_specs, check_vma=False
    )
```

```python
import math

import jax
import jax.numpy as jnp
from jax import lax
from jax.experimental import pallas as pl
from jax.experimental.pallas import tpu as pltpu
from jax.sharding import Mesh
from jax.sharding import PartitionSpec as P

D = 5120
R = 256
NZ, NX, NC, NY = 8, 4, 2, 4
FSDP = ("z", "x", "c")
TOKENS = 128
ROWS = D // (NZ * NX * NC)
COLS = D // NY
HALF = COLS // NC
PAIR = NZ // NY
STEP = 128
EDGE = 64
GROUP = 8
BLOCKS = R // EDGE
F32 = jnp.float32

momentum_decay = 0.95


def shape(*dims):
    return jax.ShapeDtypeStruct(dims, F32)


def shifted(v, axis, n, k):
    return lax.ppermute(v, axis, [(i, (i + k) % n) for i in range(n)])


def other_core(v):
    return lax.ppermute(v, "c", [(0, 1), (1, 0)])


def over_tp(v):
    total = v
    for k in range(1, NY):
        total = total + shifted(v, "tp", NY, k)
    return total


def plain(a, b, dims):
    return lax.dot_general(a, b, (dims, ((), ())), preferred_element_type=F32)


def full(a, b, dims):
    return lax.dot_general(
        a, b, (dims, ((), ())), precision=lax.Precision.HIGHEST, preferred_element_type=F32
    )


def near_dot(a, b, dims):
    return lax.dot_general(
        a, b, (dims, ((), ())), precision=lax.Precision.HIGH, preferred_element_type=F32
    )


def call(kernel, scalars, out_shape, in_specs, *args, out_specs=None, grid=(1,), scratch=()):
    if out_specs is None:
        leaves = out_shape if isinstance(out_shape, tuple) else (out_shape,)
        specs = tuple(whole(s.shape) for s in leaves)
        out_specs = specs if isinstance(out_shape, tuple) else specs[0]
    return pl.pallas_call(
        kernel,
        out_shape=out_shape,
        grid_spec=pltpu.PrefetchScalarGridSpec(
            num_scalar_prefetch=1,
            grid=grid,
            in_specs=in_specs,
            out_specs=out_specs,
            scratch_shapes=scratch,
        ),
    )(scalars, *args)


def whole(dims):
    zeros = (0,) * len(dims)
    return pl.BlockSpec(tuple(dims), lambda i, at: zeros)


C, T, X = range(3)


def gram_kernel(at, near, far, out):
    out[...] = jnp.zeros((R, R), F32)

    def step(i, _):
        here = pl.ds(pl.multiple_of(i * STEP, STEP), STEP)
        block = jnp.concatenate([near[here, :], far[here, :]], axis=0)
        out[...] += full(block, block, ((0,), (0,)))
        return 0

    lax.fori_loop(0, HALF // STEP, step, 0)


def turn_kernel(at, outs, out):
    out[...] = outs[...].astype(F32).T.reshape(NX, 1, NC * ROWS, TOKENS)


def factor_kernel(at, work_in, done, work_ref, out_ref):
    work_ref[...] = work_in[...]
    out_ref[...] = done[...]
    rows = lax.broadcasted_iota(jnp.int32, (EDGE, 2 * EDGE), 0)
    lanes = lax.broadcasted_iota(jnp.int32, (EDGE, 2 * EDGE), 1)
    eye = (rows + EDGE == lanes).astype(F32)
    rest_lanes = lax.broadcasted_iota(jnp.int32, (EDGE, R), 1)

    def step(j, _):
        i = at[0] + j
        here = pl.ds(pl.multiple_of(i * EDGE, EDGE), EDGE)
        state = jnp.where(lanes < EDGE, work_ref[here, : 2 * EDGE], eye)
        pivots = jnp.zeros((EDGE, 2 * EDGE), F32)

        def group(g, carry):
            state, pivots = carry
            live = rows < EDGE - GROUP * g
            for k in range(GROUP):
                column = jnp.broadcast_to(state[:, k : k + 1], (EDGE, 2 * EDGE))
                pivot = column[k : k + 1, :]
                line = state[k : k + 1, :] / pivot
                pivots = jnp.where(rows == k, jnp.broadcast_to(pivot, rows.shape), pivots)
                state = state - jnp.where((rows > k) & live, column, 0.0) * line
            state = jnp.concatenate([state[GROUP:], state[:GROUP]], axis=0)
            pivots = jnp.concatenate([pivots[GROUP:], pivots[:GROUP]], axis=0)
            return pltpu.roll(state, 2 * EDGE - GROUP, 1), pivots

        state, pivots = lax.fori_loop(0, EDGE // GROUP, group, (state, pivots))
        inverse = (state * lax.rsqrt(pivots))[:, :EDGE]
        upper = full(inverse, work_ref[here, :], ((1,), (0,)))
        out_ref[here, :] = pltpu.roll(upper, i * EDGE, 1)[:, R:]
        rest = jnp.where(rest_lanes < (BLOCKS - i) * EDGE, upper[:, :R], 0.0)
        change = full(rest, upper, ((0,), (0,)))
        for r in range(1, BLOCKS):
            there = pl.ds(pl.multiple_of(((i + r) % BLOCKS) * EDGE, EDGE), EDGE)
            left = work_ref[there, :] - change[r * EDGE : (r + 1) * EDGE, :]
            work_ref[there, :] = pltpu.roll(left, 2 * R - EDGE, 1)
        return 0

    lax.fori_loop(0, at[1], step, 0)


def factor_step(first_block, count, work, done):
    return call(
        factor_kernel, jnp.array([first_block, count], jnp.int32),
        (shape(R, 2 * R), shape(R, R)), [whole((R, 2 * R)), whole((R, R))], work, done,
    )


def product_kernel(at, *refs):
    sources, (acts, kept, given, joined, lhs) = refs[:NY], refs[NY:]

    @pl.when(pl.program_id(0) == 0)
    def _():
        for k in range(NX):
            here = pl.ds(pl.multiple_of(((at[X] - k) & (NX - 1)) * TOKENS, TOKENS), TOKENS)
            joined[k * TOKENS : (k + 1) * TOKENS, :] = acts[here, :].astype(jnp.bfloat16)

    for j, source in enumerate(sources):

        @pl.when(((at[T] - pl.program_id(0)) & (NY - 1)) == j)
        def _():
            for k in range(NX):
                lhs[:, k * TOKENS : (k + 1) * TOKENS] = source[k].astype(jnp.bfloat16)

    first = at[C] == 0

    def columns(n, _):
        here = pl.ds(pl.multiple_of(n * 2 * STEP, STEP), 2 * STEP)
        total = plain(lhs[...], joined[:, here], ((1,), (0,)))
        for i in range(PAIR):
            near = total[NC * i * ROWS : (NC * i + 1) * ROWS]
            far = total[(NC * i + 1) * ROWS : (NC * i + 2) * ROWS]
            kept[i * ROWS : (i + 1) * ROWS, here] = jnp.where(first, near, far)
            given[i * ROWS : (i + 1) * ROWS, here] = jnp.where(first, far, near)
        return 0

    lax.fori_loop(0, COLS // (2 * STEP), columns, 0)


def core_products(at, outs, acts):
    half = shape(NZ * ROWS, COLS)
    half_spec = pl.BlockSpec((PAIR * ROWS, COLS), lambda i, at: (i, 0))
    return call(
        product_kernel, at, (half, half),
        [whole(v.shape) for v in outs] + [whole(acts.shape)], *outs, acts,
        out_specs=(half_spec, half_spec), grid=(NY,),
        scratch=[
            pltpu.VMEM(acts.shape, jnp.bfloat16),
            pltpu.VMEM((PAIR * NC * ROWS, NX * TOKENS), jnp.bfloat16),
        ],
    )


def summed_piece(kept, given):
    pieces = (kept + other_core(given)).reshape(NX, HALF // NX, R)
    arrived = lax.all_to_all(pieces, "x", 0, 0, tiled=True)
    pieces = jnp.sum(arrived, axis=0).reshape(NZ, HALF // (NX * NZ), R)
    arrived = lax.all_to_all(pieces, "z", 0, 0, tiled=True)
    return jnp.sum(arrived, axis=0)


def spread_over(v, axis, n):
    copies = jnp.broadcast_to(v[None], (n, *v.shape))
    return lax.all_to_all(copies, axis, 0, 0, tiled=True).reshape(-1, v.shape[1])


def gathered(piece):
    part = spread_over(piece, "z", NZ)
    near = spread_over(part, "x", NX)
    return near, other_core(near)


def on_device(activations, out_grad, momentum, right_prev):
    z, x, c = lax.axis_index("z"), lax.axis_index("x"), lax.axis_index("c")
    t = lax.axis_index("tp")
    mine = (z * NX + x) * NC + c
    at = jnp.stack([c, t, x]).astype(jnp.int32)

    held = jnp.concatenate([activations.astype(F32), momentum])
    first = near_dot(held, right_prev, ((1,), (0,)))
    first, activations, out_grad = lax.optimization_barrier((first, activations, out_grad))
    first = over_tp(first)

    acts = lax.all_gather(activations.astype(F32), "x", axis=0, tiled=True)
    turned = call(
        turn_kernel, at, shape(NX, PAIR, NC * ROWS, TOKENS),
        [pl.BlockSpec((TOKENS, D // NZ), lambda i, at: (0, PAIR * at[T] + i))], out_grad,
        out_specs=pl.BlockSpec((NX, 1, NC * ROWS, TOKENS), lambda i, at: (0, i, 0, 0)),
        grid=(PAIR,),
    )
    turned = turned.reshape(NX, PAIR * NC * ROWS, TOKENS)
    outs = []
    for k in range(NX):
        block = lax.dynamic_index_in_dim(turned, (x + k) & (NX - 1), 0, keepdims=False)
        outs.append(shifted(block, "x", NX, k) if k else block)
    outs = jnp.stack(outs)
    outs = [outs] + [shifted(outs, "tp", NY, k) for k in range(1, NY)]

    helds, spreads = [], []
    for half in (c, 1 - c):
        helds.append(lax.dynamic_slice_in_dim(held, half * HALF, HALF, 1))
        start = t * COLS + half * HALF
        place = lax.broadcasted_iota(jnp.int32, (ROWS, HALF), 0) + (mine * ROWS - start)
        place = place == lax.broadcasted_iota(jnp.int32, (ROWS, HALF), 1)
        part = lax.dynamic_slice_in_dim(out_grad, start, HALF, 1)
        spreads.append(jnp.concatenate([part.astype(F32), place.astype(F32)]))

    given = near_dot(spreads[1], first, ((0,), (0,)))
    kept = near_dot(spreads[0], first, ((0,), (0,)))
    piece = summed_piece(kept, given)
    near, far = gathered(piece)
    seen = near_dot(spreads[0], near, ((1,), (0,))) + near_dot(spreads[1], far, ((1,), (0,)))
    seen, at_seen = lax.optimization_barrier((seen, at))
    kept_grad, given_grad = core_products(at_seen, outs, acts)
    summed_grad = kept_grad + other_core(given_grad)
    grad = lax.psum_scatter(summed_grad, "z", scatter_dimension=0, tiled=True)
    second = over_tp(seen)

    gram = call(gram_kernel, at, shape(R, R), [whole((HALF, R))] * 2, near, far)
    gram, second = lax.optimization_barrier((gram, second))
    gram = over_tp(gram)

    given = near_dot(helds[1], second, ((0,), (0,)))
    kept = near_dot(helds[0], second, ((0,), (0,)))
    piece = summed_piece(kept, given)
    work = jnp.concatenate([gram, jnp.eye(R, dtype=F32)], axis=1)
    work, done = factor_step(0, 2, work, jnp.zeros((R, R), F32))
    near, far = gathered(piece)
    work, done = factor_step(2, 1, work, done)
    _, inverse = factor_step(3, 1, work, done)
    basis = near_dot(second[TOKENS:], inverse, ((1,), (1,)))
    rights = [near_dot(v, inverse, ((1,), (1,))) for v in (near, far)]
    squares = sum(jnp.sum(v * v, axis=0) for v in rights)
    squares = over_tp(jnp.broadcast_to(squares[None], (8, R)))[:1]
    factor = lax.rsqrt(squares / D + 1e-06)

    def in_order(pair, axis):
        return jnp.concatenate(
            [jnp.where(c == 0, pair[0], pair[1]), jnp.where(c == 0, pair[1], pair[0])], axis=axis
        )

    change = in_order([near_dot(basis, v, ((1,), (1,))) for v in rights], 1)
    update = in_order([near_dot(basis * factor, v, ((1,), (1,))) for v in rights], 1)
    new_momentum = (momentum + grad) - (1.0 - momentum_decay) * change
    own = R // (NZ * NX * NC)
    owned = in_order([lax.dynamic_slice_in_dim(v, mine * own, own, 1) for v in rights], 0)
    owned = owned * lax.dynamic_slice_in_dim(factor, mine * own, own, 1)
    return (new_momentum, math.sqrt(D / R) * update, owned)


def solution(mesh):
    finer = Mesh(mesh.devices.reshape(NZ, NX, NC, mesh.shape["tp"]), ("z", "x", "c", "tp"))
    in_specs = (P(FSDP, "tp"), P(FSDP, None), P(FSDP, "tp"), P("tp", None))
    out_specs = (P(FSDP, "tp"), P(FSDP, "tp"), P("tp", FSDP))
    return jax.shard_map(
        on_device, mesh=finer, in_specs=in_specs, out_specs=out_specs, check_vma=False
    )
```

```python
import math

import jax
import jax.numpy as jnp
from jax import lax
from jax.experimental import pallas as pl
from jax.experimental.pallas import tpu as pltpu
from jax.sharding import Mesh
from jax.sharding import PartitionSpec as P

D = 5120
R = 256
NZ, NX, NC, NY = 8, 4, 2, 4
FSDP = ("z", "x", "c")
TOKENS = 128
ROWS = D // (NZ * NX * NC)
COLS = D // NY
HALF = COLS // NC
PAIR = NZ // NY
STEP = 128
EDGE = 64
GROUP = 8
BLOCKS = R // EDGE
F32 = jnp.float32

momentum_decay = 0.95


def shape(*dims):
    return jax.ShapeDtypeStruct(dims, F32)


def shifted(v, axis, n, k):
    return lax.ppermute(v, axis, [(i, (i + k) % n) for i in range(n)])


def other_core(v):
    return lax.ppermute(v, "c", [(0, 1), (1, 0)])


def over_tp(v):
    total = v
    for k in range(1, NY):
        total = total + shifted(v, "tp", NY, k)
    return total


def plain(a, b, dims):
    return lax.dot_general(a, b, (dims, ((), ())), preferred_element_type=F32)


def full(a, b, dims):
    return lax.dot_general(
        a, b, (dims, ((), ())), precision=lax.Precision.HIGHEST, preferred_element_type=F32
    )


def near_dot(a, b, dims):
    return lax.dot_general(
        a, b, (dims, ((), ())), precision=lax.Precision.HIGH, preferred_element_type=F32
    )


def call(kernel, scalars, out_shape, in_specs, *args, out_specs=None, grid=(1,), scratch=()):
    if out_specs is None:
        leaves = out_shape if isinstance(out_shape, tuple) else (out_shape,)
        specs = tuple(whole(s.shape) for s in leaves)
        out_specs = specs if isinstance(out_shape, tuple) else specs[0]
    return pl.pallas_call(
        kernel,
        out_shape=out_shape,
        grid_spec=pltpu.PrefetchScalarGridSpec(
            num_scalar_prefetch=1,
            grid=grid,
            in_specs=in_specs,
            out_specs=out_specs,
            scratch_shapes=scratch,
        ),
    )(scalars, *args)


def whole(dims):
    zeros = (0,) * len(dims)
    return pl.BlockSpec(tuple(dims), lambda i, at: zeros)


C, T, X = range(3)


def gram_kernel(at, near, far, out):
    out[...] = jnp.zeros((R, R), F32)

    def step(i, _):
        here = pl.ds(pl.multiple_of(i * STEP, STEP), STEP)
        block = jnp.concatenate([near[here, :], far[here, :]], axis=0)
        out[...] += full(block, block, ((0,), (0,)))
        return 0

    lax.fori_loop(0, HALF // STEP, step, 0)


def turn_kernel(at, outs, out):
    out[...] = outs[...].astype(F32).T.reshape(NX, 1, NC * ROWS, TOKENS)


def factor_kernel(at, work_in, done, work_ref, out_ref):
    work_ref[...] = work_in[...]
    out_ref[...] = done[...]
    rows = lax.broadcasted_iota(jnp.int32, (EDGE, 2 * EDGE), 0)
    lanes = lax.broadcasted_iota(jnp.int32, (EDGE, 2 * EDGE), 1)
    eye = (rows + EDGE == lanes).astype(F32)
    rest_lanes = lax.broadcasted_iota(jnp.int32, (EDGE, R), 1)

    def step(j, _):
        i = at[0] + j
        here = pl.ds(pl.multiple_of(i * EDGE, EDGE), EDGE)
        state = jnp.where(lanes < EDGE, work_ref[here, : 2 * EDGE], eye)
        pivots = jnp.zeros((EDGE, 2 * EDGE), F32)

        def group(g, carry):
            state, pivots = carry
            columns = [jnp.broadcast_to(state[:, j : j + 1], rows.shape) for j in range(GROUP)]
            heads = [state[j : j + 1, :] for j in range(GROUP)]
            found = []
            for j in range(GROUP):
                pivot = columns[j][j : j + 1, :]
                found.append(pivot)
                inverse = 1.0 / pivot
                line = heads[j] * inverse
                for i in range(j + 1, GROUP):
                    heads[i] = heads[i] - columns[j][i : i + 1, :] * line
                    columns[i] = columns[i] - columns[j] * (columns[i][j : j + 1, :] * inverse)
                below = jnp.where(rows[:GROUP] > j, columns[j][:GROUP], 0.0)
                state = state - jnp.concatenate([below, columns[j][GROUP:]], axis=0) * line
            head = jnp.where(lanes[:GROUP] < EDGE - GROUP * g, 0.0, state[:GROUP])
            state = jnp.concatenate([state[GROUP:], head], axis=0)
            pivots = jnp.concatenate([pivots[GROUP:], *found], axis=0)
            return pltpu.roll(state, 2 * EDGE - GROUP, 1), pivots

        state, pivots = lax.fori_loop(0, EDGE // GROUP, group, (state, pivots))
        inverse = (state * lax.rsqrt(pivots))[:, :EDGE]
        upper = full(inverse, work_ref[here, :], ((1,), (0,)))
        out_ref[here, :] = pltpu.roll(upper, i * EDGE, 1)[:, R:]
        rest = jnp.where(rest_lanes < (BLOCKS - i) * EDGE, upper[:, :R], 0.0)
        change = full(rest, upper, ((0,), (0,)))
        for r in range(1, BLOCKS):
            there = pl.ds(pl.multiple_of(((i + r) % BLOCKS) * EDGE, EDGE), EDGE)
            left = work_ref[there, :] - change[r * EDGE : (r + 1) * EDGE, :]
            work_ref[there, :] = pltpu.roll(left, 2 * R - EDGE, 1)
        return 0

    lax.fori_loop(0, at[1], step, 0)


def factor_step(first_block, count, work, done):
    return call(
        factor_kernel, jnp.array([first_block, count], jnp.int32),
        (shape(R, 2 * R), shape(R, R)), [whole((R, 2 * R)), whole((R, R))], work, done,
    )


def product_kernel(at, *refs):
    sources, (acts, kept, given, joined, lhs) = refs[:NY], refs[NY:]

    @pl.when(pl.program_id(0) == 0)
    def _():
        for k in range(NX):
            here = pl.ds(pl.multiple_of(((at[X] - k) & (NX - 1)) * TOKENS, TOKENS), TOKENS)
            joined[k * TOKENS : (k + 1) * TOKENS, :] = acts[here, :].astype(jnp.bfloat16)

    for j, source in enumerate(sources):

        @pl.when(((at[T] - pl.program_id(0)) & (NY - 1)) == j)
        def _():
            for k in range(NX):
                lhs[:, k * TOKENS : (k + 1) * TOKENS] = source[k].astype(jnp.bfloat16)

    total = plain(lhs[...], joined[...], ((1,), (0,)))
    first = at[C] == 0
    for i in range(PAIR):
        near = total[NC * i * ROWS : (NC * i + 1) * ROWS]
        far = total[(NC * i + 1) * ROWS : (NC * i + 2) * ROWS]
        kept[i * ROWS : (i + 1) * ROWS, :] = jnp.where(first, near, far)
        given[i * ROWS : (i + 1) * ROWS, :] = jnp.where(first, far, near)


def core_products(at, outs, acts):
    half = shape(NZ * ROWS, COLS)
    half_spec = pl.BlockSpec((PAIR * ROWS, COLS), lambda i, at: (i, 0))
    return call(
        product_kernel, at, (half, half),
        [whole(v.shape) for v in outs] + [whole(acts.shape)], *outs, acts,
        out_specs=(half_spec, half_spec), grid=(NY,),
        scratch=[
            pltpu.VMEM(acts.shape, jnp.bfloat16),
            pltpu.VMEM((PAIR * NC * ROWS, NX * TOKENS), jnp.bfloat16),
        ],
    )


def summed_at_once(kept, given):
    pieces = (kept + other_core(given)).reshape(NX * NZ, HALF // (NX * NZ), R)
    arrived = lax.all_to_all(pieces, ("x", "z"), 0, 0, tiled=True)
    return jnp.sum(arrived, axis=0)


def summed_in_turn(kept, given):
    pieces = (kept + other_core(given)).reshape(NX, HALF // NX, R)
    arrived = lax.all_to_all(pieces, "x", 0, 0, tiled=True)
    pieces = jnp.sum(arrived, axis=0).reshape(NZ, HALF // (NX * NZ), R)
    arrived = lax.all_to_all(pieces, "z", 0, 0, tiled=True)
    return jnp.sum(arrived, axis=0)


def spread_over(v, axis, n):
    copies = jnp.broadcast_to(v[None], (n, *v.shape))
    return lax.all_to_all(copies, axis, 0, 0, tiled=True).reshape(-1, v.shape[1])


def gathered(piece):
    part = spread_over(piece, "z", NZ)
    near = spread_over(part, "x", NX)
    return near, other_core(near)


def on_device(activations, out_grad, momentum, right_prev):
    z, x, c = lax.axis_index("z"), lax.axis_index("x"), lax.axis_index("c")
    t = lax.axis_index("tp")
    mine = (z * NX + x) * NC + c
    at = jnp.stack([c, t, x]).astype(jnp.int32)

    held = jnp.concatenate([activations.astype(F32), momentum])
    first = near_dot(held, right_prev, ((1,), (0,)))
    first, activations, out_grad = lax.optimization_barrier((first, activations, out_grad))
    first = over_tp(first)

    acts = lax.all_gather(activations.astype(F32), "x", axis=0, tiled=True)
    turned = call(
        turn_kernel, at, shape(NX, PAIR, NC * ROWS, TOKENS),
        [pl.BlockSpec((TOKENS, D // NZ), lambda i, at: (0, PAIR * at[T] + i))], out_grad,
        out_specs=pl.BlockSpec((NX, 1, NC * ROWS, TOKENS), lambda i, at: (0, i, 0, 0)),
        grid=(PAIR,),
    )
    turned = turned.reshape(NX, PAIR * NC * ROWS, TOKENS)
    outs = []
    for k in range(NX):
        block = lax.dynamic_index_in_dim(turned, (x + k) & (NX - 1), 0, keepdims=False)
        outs.append(shifted(block, "x", NX, k) if k else block)
    outs = jnp.stack(outs)
    outs = [outs] + [shifted(outs, "tp", NY, k) for k in range(1, NY)]

    helds, spreads = [], []
    for half in (c, 1 - c):
        helds.append(lax.dynamic_slice_in_dim(held, half * HALF, HALF, 1))
        start = t * COLS + half * HALF
        place = lax.broadcasted_iota(jnp.int32, (ROWS, HALF), 0) + (mine * ROWS - start)
        place = place == lax.broadcasted_iota(jnp.int32, (ROWS, HALF), 1)
        part = lax.dynamic_slice_in_dim(out_grad, start, HALF, 1)
        spreads.append(jnp.concatenate([part.astype(F32), place.astype(F32)]))

    given = near_dot(spreads[1], first, ((0,), (0,)))
    kept = near_dot(spreads[0], first, ((0,), (0,)))
    piece = summed_at_once(kept, given)
    piece, at_left = lax.optimization_barrier((piece, at))
    kept_grad, given_grad = core_products(at_left, outs, acts)
    near, far = gathered(piece)
    seen = near_dot(spreads[0], near, ((1,), (0,))) + near_dot(spreads[1], far, ((1,), (0,)))
    summed_grad = kept_grad + other_core(given_grad)
    grad = lax.psum_scatter(summed_grad, "z", scatter_dimension=0, tiled=True)
    second = over_tp(seen)

    gram = call(gram_kernel, at, shape(R, R), [whole((HALF, R))] * 2, near, far)
    gram, second = lax.optimization_barrier((gram, second))
    gram = over_tp(gram)

    given = near_dot(helds[1], second, ((0,), (0,)))
    kept = near_dot(helds[0], second, ((0,), (0,)))
    piece = summed_in_turn(kept, given)
    work = jnp.concatenate([gram, jnp.eye(R, dtype=F32)], axis=1)
    work, done = factor_step(0, 2, work, jnp.zeros((R, R), F32))
    near, far = gathered(piece)
    _, inverse = factor_step(2, 2, work, done)
    basis = near_dot(second[TOKENS:], inverse, ((1,), (1,)))
    rights = [near_dot(v, inverse, ((1,), (1,))) for v in (near, far)]
    squares = sum(jnp.sum(v * v, axis=0) for v in rights)
    squares = over_tp(jnp.broadcast_to(squares[None], (8, R)))[:1]
    factor = lax.rsqrt(squares / D + 1e-06)

    def in_order(pair, axis):
        return jnp.concatenate(
            [jnp.where(c == 0, pair[0], pair[1]), jnp.where(c == 0, pair[1], pair[0])], axis=axis
        )

    change = in_order([near_dot(basis, v, ((1,), (1,))) for v in rights], 1)
    update = in_order([near_dot(basis * factor, v, ((1,), (1,))) for v in rights], 1)
    new_momentum = (momentum + grad) - (1.0 - momentum_decay) * change
    own = R // (NZ * NX * NC)
    owned = in_order([lax.dynamic_slice_in_dim(v, mine * own, own, 1) for v in rights], 0)
    owned = owned * lax.dynamic_slice_in_dim(factor, mine * own, own, 1)
    return (new_momentum, math.sqrt(D / R) * update, owned)


def solution(mesh):
    finer = Mesh(mesh.devices.reshape(NZ, NX, NC, mesh.shape["tp"]), ("z", "x", "c", "tp"))
    in_specs = (P(FSDP, "tp"), P(FSDP, None), P(FSDP, "tp"), P("tp", None))
    out_specs = (P(FSDP, "tp"), P(FSDP, "tp"), P("tp", FSDP))
    return jax.shard_map(
        on_device, mesh=finer, in_specs=in_specs, out_specs=out_specs, check_vma=False
    )
```

```python
import math

import jax
import jax.numpy as jnp
from jax import lax
from jax.experimental import pallas as pl
from jax.experimental.pallas import tpu as pltpu
from jax.sharding import Mesh
from jax.sharding import PartitionSpec as P

D = 5120
R = 256
NZ, NX, NC, NY = 8, 4, 2, 4
FSDP = ("z", "x", "c")
TOKENS = 128
ROWS = D // (NZ * NX * NC)
COLS = D // NY
HALF = COLS // NC
PAIR = NZ // NY
STEP = 128
EDGE = 64
GROUP = 8
BLOCKS = R // EDGE
F32 = jnp.float32

momentum_decay = 0.95


def shape(*dims):
    return jax.ShapeDtypeStruct(dims, F32)


def shifted(v, axis, n, k):
    return lax.ppermute(v, axis, [(i, (i + k) % n) for i in range(n)])


def other_core(v):
    return lax.ppermute(v, "c", [(0, 1), (1, 0)])


def over_tp(v):
    total = v
    for k in range(1, NY):
        total = total + shifted(v, "tp", NY, k)
    return total


def plain(a, b, dims):
    return lax.dot_general(a, b, (dims, ((), ())), preferred_element_type=F32)


def full(a, b, dims):
    return lax.dot_general(
        a, b, (dims, ((), ())), precision=lax.Precision.HIGHEST, preferred_element_type=F32
    )


def near_dot(a, b, dims):
    return lax.dot_general(
        a, b, (dims, ((), ())), precision=lax.Precision.HIGH, preferred_element_type=F32
    )


def call(kernel, scalars, out_shape, in_specs, *args, out_specs=None, grid=(1,), scratch=()):
    if out_specs is None:
        leaves = out_shape if isinstance(out_shape, tuple) else (out_shape,)
        specs = tuple(whole(s.shape) for s in leaves)
        out_specs = specs if isinstance(out_shape, tuple) else specs[0]
    return pl.pallas_call(
        kernel,
        out_shape=out_shape,
        grid_spec=pltpu.PrefetchScalarGridSpec(
            num_scalar_prefetch=1,
            grid=grid,
            in_specs=in_specs,
            out_specs=out_specs,
            scratch_shapes=scratch,
        ),
    )(scalars, *args)


def whole(dims):
    zeros = (0,) * len(dims)
    return pl.BlockSpec(tuple(dims), lambda i, at: zeros)


C, T, X = range(3)


def gram_kernel(at, near, far, out):
    out[...] = jnp.zeros((R, R), F32)

    def step(i, _):
        here = pl.ds(pl.multiple_of(i * STEP, STEP), STEP)
        block = jnp.concatenate([near[here, :], far[here, :]], axis=0)
        out[...] += full(block, block, ((0,), (0,)))
        return 0

    lax.fori_loop(0, HALF // STEP, step, 0)


def turn_kernel(at, outs, out):
    out[...] = outs[...].astype(F32).T.reshape(NX, 1, NC * ROWS, TOKENS)


def factor_kernel(at, work_in, done, work_ref, out_ref):
    work_ref[...] = work_in[...]
    out_ref[...] = done[...]
    rows = lax.broadcasted_iota(jnp.int32, (EDGE, 2 * EDGE), 0)
    lanes = lax.broadcasted_iota(jnp.int32, (EDGE, 2 * EDGE), 1)
    eye = (rows + EDGE == lanes).astype(F32)
    rest_lanes = lax.broadcasted_iota(jnp.int32, (EDGE, R), 1)

    def step(j, _):
        i = at[0] + j
        here = pl.ds(pl.multiple_of(i * EDGE, EDGE), EDGE)
        state = jnp.where(lanes < EDGE, work_ref[here, : 2 * EDGE], eye)
        pivots = jnp.zeros((EDGE, 2 * EDGE), F32)

        def group(g, carry):
            state, pivots = carry
            columns = [jnp.broadcast_to(state[:, j : j + 1], rows.shape) for j in range(GROUP)]
            heads = [state[j : j + 1, :] for j in range(GROUP)]
            found = []
            for j in range(GROUP):
                pivot = columns[j][j : j + 1, :]
                found.append(pivot)
                inverse = 1.0 / pivot
                line = heads[j] * inverse
                for i in range(j + 1, GROUP):
                    heads[i] = heads[i] - columns[j][i : i + 1, :] * line
                    columns[i] = columns[i] - columns[j] * (columns[i][j : j + 1, :] * inverse)
                below = jnp.where(rows[:GROUP] > j, columns[j][:GROUP], 0.0)
                state = state - jnp.concatenate([below, columns[j][GROUP:]], axis=0) * line
            head = jnp.where(lanes[:GROUP] < EDGE - GROUP * g, 0.0, state[:GROUP])
            state = jnp.concatenate([state[GROUP:], head], axis=0)
            pivots = jnp.concatenate([pivots[GROUP:], *found], axis=0)
            return pltpu.roll(state, 2 * EDGE - GROUP, 1), pivots

        state, pivots = lax.fori_loop(0, EDGE // GROUP, group, (state, pivots))
        inverse = (state * lax.rsqrt(pivots))[:, :EDGE]
        upper = full(inverse, work_ref[here, :], ((1,), (0,)))
        out_ref[here, :] = pltpu.roll(upper, i * EDGE, 1)[:, R:]
        rest = jnp.where(rest_lanes < (BLOCKS - i) * EDGE, upper[:, :R], 0.0)
        change = full(rest, upper, ((0,), (0,)))
        for r in range(1, BLOCKS):
            there = pl.ds(pl.multiple_of(((i + r) % BLOCKS) * EDGE, EDGE), EDGE)
            left = work_ref[there, :] - change[r * EDGE : (r + 1) * EDGE, :]
            work_ref[there, :] = pltpu.roll(left, 2 * R - EDGE, 1)
        return 0

    lax.fori_loop(0, at[1], step, 0)


def factor_step(first_block, count, work, done):
    return call(
        factor_kernel, jnp.array([first_block, count], jnp.int32),
        (shape(R, 2 * R), shape(R, R)), [whole((R, 2 * R)), whole((R, R))], work, done,
    )


def product_kernel(at, *refs):
    sources, (acts, kept, given, joined, lhs) = refs[:NY], refs[NY:]

    @pl.when(pl.program_id(0) == 0)
    def _():
        for k in range(NX):
            here = pl.ds(pl.multiple_of(((at[X] - k) & (NX - 1)) * TOKENS, TOKENS), TOKENS)
            joined[k * TOKENS : (k + 1) * TOKENS, :] = acts[here, :].astype(jnp.bfloat16)

    for j, source in enumerate(sources):

        @pl.when(((at[T] - pl.program_id(0)) & (NY - 1)) == j)
        def _():
            for k in range(NX):
                lhs[:, k * TOKENS : (k + 1) * TOKENS] = source[k].astype(jnp.bfloat16)

    total = plain(lhs[...], joined[...], ((1,), (0,)))
    first = at[C] == 0
    for i in range(PAIR):
        near = total[NC * i * ROWS : (NC * i + 1) * ROWS]
        far = total[(NC * i + 1) * ROWS : (NC * i + 2) * ROWS]
        kept[i * ROWS : (i + 1) * ROWS, :] = jnp.where(first, near, far)
        given[i * ROWS : (i + 1) * ROWS, :] = jnp.where(first, far, near)


def core_products(at, outs, acts):
    half = shape(NZ * ROWS, COLS)
    half_spec = pl.BlockSpec((PAIR * ROWS, COLS), lambda i, at: (i, 0))
    return call(
        product_kernel, at, (half, half),
        [whole(v.shape) for v in outs] + [whole(acts.shape)], *outs, acts,
        out_specs=(half_spec, half_spec), grid=(NY,),
        scratch=[
            pltpu.VMEM(acts.shape, jnp.bfloat16),
            pltpu.VMEM((PAIR * NC * ROWS, NX * TOKENS), jnp.bfloat16),
        ],
    )


def summed_at_once(kept, given):
    pieces = (kept + other_core(given)).reshape(NX * NZ, HALF // (NX * NZ), R)
    arrived = lax.all_to_all(pieces, ("x", "z"), 0, 0, tiled=True)
    return jnp.sum(arrived, axis=0)


def summed_in_turn(kept, given):
    pieces = (kept + other_core(given)).reshape(NX, HALF // NX, R)
    arrived = lax.all_to_all(pieces, "x", 0, 0, tiled=True)
    pieces = jnp.sum(arrived, axis=0).reshape(NZ, HALF // (NX * NZ), R)
    arrived = lax.all_to_all(pieces, "z", 0, 0, tiled=True)
    return jnp.sum(arrived, axis=0)


def spread_over(v, axis, n):
    copies = jnp.broadcast_to(v[None], (n, *v.shape))
    return lax.all_to_all(copies, axis, 0, 0, tiled=True).reshape(-1, v.shape[1])


def gathered(piece):
    part = spread_over(piece, "z", NZ)
    near = spread_over(part, "x", NX)
    return near, other_core(near)


def on_device(activations, out_grad, momentum, right_prev):
    z, x, c = lax.axis_index("z"), lax.axis_index("x"), lax.axis_index("c")
    t = lax.axis_index("tp")
    mine = (z * NX + x) * NC + c
    at = jnp.stack([c, t, x]).astype(jnp.int32)

    held = jnp.concatenate([activations.astype(F32), momentum])
    first = near_dot(held, right_prev, ((1,), (0,)))
    first, activations, out_grad = lax.optimization_barrier((first, activations, out_grad))
    first = over_tp(first)

    acts = lax.all_gather(activations.astype(F32), "x", axis=0, tiled=True)
    turned = call(
        turn_kernel, at, shape(NX, PAIR, NC * ROWS, TOKENS),
        [pl.BlockSpec((TOKENS, D // NZ), lambda i, at: (0, PAIR * at[T] + i))], out_grad,
        out_specs=pl.BlockSpec((NX, 1, NC * ROWS, TOKENS), lambda i, at: (0, i, 0, 0)),
        grid=(PAIR,),
    )
    turned = turned.reshape(NX, PAIR * NC * ROWS, TOKENS)
    outs = []
    for k in range(NX):
        block = lax.dynamic_index_in_dim(turned, (x + k) & (NX - 1), 0, keepdims=False)
        outs.append(shifted(block, "x", NX, k) if k else block)
    outs = jnp.stack(outs)
    outs = [outs] + [shifted(outs, "tp", NY, k) for k in range(1, NY)]

    helds, spreads = [], []
    for half in (c, 1 - c):
        helds.append(lax.dynamic_slice_in_dim(held, half * HALF, HALF, 1))
        start = t * COLS + half * HALF
        place = lax.broadcasted_iota(jnp.int32, (ROWS, HALF), 0) + (mine * ROWS - start)
        place = place == lax.broadcasted_iota(jnp.int32, (ROWS, HALF), 1)
        part = lax.dynamic_slice_in_dim(out_grad, start, HALF, 1)
        spreads.append(jnp.concatenate([part.astype(F32), place.astype(F32)]))

    given = near_dot(spreads[1], first, ((0,), (0,)))
    kept = near_dot(spreads[0], first, ((0,), (0,)))
    piece = summed_at_once(kept, given)
    piece, at_left = lax.optimization_barrier((piece, at))
    kept_grad, given_grad = core_products(at_left, outs, acts)
    near, far = gathered(piece)
    seen = near_dot(spreads[0], near, ((1,), (0,))) + near_dot(spreads[1], far, ((1,), (0,)))
    summed_grad = kept_grad + other_core(given_grad)
    grad = lax.psum_scatter(summed_grad, "z", scatter_dimension=0, tiled=True)
    second = over_tp(seen)

    gram = call(gram_kernel, at, shape(R, R), [whole((HALF, R))] * 2, near, far)
    gram, second = lax.optimization_barrier((gram, second))
    gram = over_tp(gram)

    given = near_dot(helds[1], second, ((0,), (0,)))
    kept = near_dot(helds[0], second, ((0,), (0,)))
    piece = summed_in_turn(kept, given)
    identity = jnp.eye(R, dtype=F32)
    work = jnp.concatenate([gram, identity], axis=1)
    work, done = factor_step(0, 2, work, identity)
    near, far = gathered(piece)
    _, inverse = factor_step(2, 2, work, done)
    basis = near_dot(second[TOKENS:], inverse, ((1,), (1,)))
    rights = [near_dot(v, inverse, ((1,), (1,))) for v in (near, far)]
    squares = sum(jnp.sum(v * v, axis=0) for v in rights)
    squares = over_tp(jnp.broadcast_to(squares[None], (8, R)))[:1]
    factor = lax.rsqrt(squares / D + 1e-06)

    def in_order(pair, axis):
        return jnp.concatenate(
            [jnp.where(c == 0, pair[0], pair[1]), jnp.where(c == 0, pair[1], pair[0])], axis=axis
        )

    change = in_order([near_dot(basis, v, ((1,), (1,))) for v in rights], 1)
    update = in_order([near_dot(basis * factor, v, ((1,), (1,))) for v in rights], 1)
    new_momentum = (momentum + grad) - (1.0 - momentum_decay) * change
    own = R // (NZ * NX * NC)
    owned = in_order([lax.dynamic_slice_in_dim(v, mine * own, own, 1) for v in rights], 0)
    owned = owned * lax.dynamic_slice_in_dim(factor, mine * own, own, 1)
    return (new_momentum, math.sqrt(D / R) * update, owned)


def solution(mesh):
    finer = Mesh(mesh.devices.reshape(NZ, NX, NC, mesh.shape["tp"]), ("z", "x", "c", "tp"))
    in_specs = (P(FSDP, "tp"), P(FSDP, None), P(FSDP, "tp"), P("tp", None))
    out_specs = (P(FSDP, "tp"), P(FSDP, "tp"), P("tp", FSDP))
    return jax.shard_map(
        on_device, mesh=finer, in_specs=in_specs, out_specs=out_specs, check_vma=False
    )
```
